32 devices in a mesh: member: 8 (over y, x, core), region: 4 (over z).
Axes of the slice: x: 2, y: 2, z: 4, core: 2. Of those that a mesh axis runs over, the one named last changes fastest.
Arguments:
- state: float32 [256, 8, 4096], P('member', None, 'region'), may hold values from -6 to 6
- adjacent_columns: int32 [6, 4096], P(None, 'region'), may hold values from 0 to 4095, as said below
- adjacent_rates: float32 [6, 4096], P(None, 'region'), may hold values from 0.02 to 0.16
- amplification_speed: float32 [4096], P('region'), may hold values from 0.05 to 0.5
- obs_patch: int32 [8192], P(('member', 'region')), may hold values from -1 to 31, as said below
- obs_row: int32 [8192], P(('member', 'region')), may hold values from 0 to 1023
- obs_value: float32 [8192], P(('member', 'region')), may hold values from -6 to 6
- obs_error: float32 [8192], P(('member', 'region')), may hold values from 0.5 to 2
Outputs:
- analysis: bfloat16 [256, 8, 4096], P('member', None, 'region')
The draws below stay inside these ranges and needn't reach their ends.
Inputs may be any that keep to these rules, and one draw needn't show every extreme that they name: `adjacent_columns`: each neighbour lies within 256 positions of its column along the closed order of columns (index modulo 4096) and is never the column itself. `obs_patch`: at most 256 rows name one patch. Within the 256 rows of one device, at most 8 rows name any one patch; -1 marks a row without an observation.
All inputs are finite; a program needn't handle non-finite values.
Results may differ from the reference program's by a relative error of at most 0.01.
Values may be sent and summed in bfloat16 or wider, within the bound.
A program may use at most 64 MiB of HBM per device.

```python
import math
import jax
import jax.numpy as jnp
from jax import lax

LEVELS = 8
PATCH_CELLS = 128
PATCH_DEV = 1
PATCH_OBS = 256
RIM = 256
STEPS = 3
NS_ITERS = 6
MEMBERS = 256
CELL_DEV = 1024
CELLS = 4096
PATCHES = 32
OBS_TOTAL = 8192
N_MEMBER = 8
N_REGION = 4


def draw_adjacent_columns(key, part):
    cells_all = CELL_DEV * N_REGION
    cell_index = jnp.arange(cells_all, dtype=jnp.int32)
    stride = jax.random.randint(jax.random.fold_in(key, 11), (6, cells_all), 1, RIM + 1)
    flips = jax.random.randint(jax.random.fold_in(key, 12), (6, cells_all), 0, 2)
    offsets = jnp.where(flips == 0, -stride, stride)
    offsets = offsets.at[0].set(jnp.where(cell_index % CELL_DEV == 0, -RIM, offsets[0]))
    offsets = offsets.at[1].set(jnp.where(cell_index % CELL_DEV == CELL_DEV - 1, RIM, offsets[1]))
    return ((cell_index[None, :] + offsets) % cells_all).astype(jnp.int32)


def draw_obs_patch(key, part):
    devices = N_MEMBER * N_REGION
    observation_shard = PATCH_DEV * PATCH_OBS
    total_rows = devices * observation_shard
    slot_position = jnp.arange(total_rows, dtype=jnp.int32)
    target = slot_position // observation_shard
    within = slot_position % observation_shard
    local_patch = within // PATCH_OBS
    shifts = jax.random.randint(jax.random.fold_in(key, 21), (devices,), 0, devices)
    source = (within + shifts[target]) % devices
    region_of = target % N_REGION
    member_of = target // N_REGION
    patch_id = region_of * (N_MEMBER * PATCH_DEV) + member_of * PATCH_DEV + local_patch
    levels_raw = jax.random.randint(jax.random.fold_in(key, 22), (devices * PATCH_DEV,), 0, 1001)
    fill_level = 100 + 900 * levels_raw * levels_raw // 1000000
    full_device = jax.random.randint(jax.random.fold_in(key, 23), (), 0, devices)
    slot_fill = jnp.where(target == full_device, 1001, fill_level[target * PATCH_DEV + local_patch])
    draws_live = jax.random.randint(jax.random.fold_in(key, 24), (total_rows,), 0, 1000)
    labelled = jnp.where(draws_live < slot_fill, patch_id, -1)
    shuffle = jax.random.permutation(jax.random.fold_in(key, 25), total_rows).astype(jnp.int32)
    ordering = jnp.argsort(source * total_rows + shuffle, stable=True)
    return labelled[ordering].astype(jnp.int32)


def set_ends(result, key, low, high):
    longest = result.shape.index(max(result.shape))
    spots = []
    for shift in (0, 1):
        where = [jax.random.randint(jax.random.fold_in(key, axis), (), 0, length) for axis, length in enumerate(result.shape)]
        where[longest] = (where[longest] + shift) % result.shape[longest]
        spots.append(tuple(where))
    return result.at[spots[0]].set(low).at[spots[1]].set(high)


def shard_levels(rng, extent, split, low, top_value):
    def one(position, shards_of):
        heights = jax.random.uniform(jax.random.fold_in(jax.random.fold_in(rng, 6), position), (shards_of,), jnp.float32, low / len(split), top_value / len(split))
        return jnp.repeat(jnp.exp(heights), extent[position] // shards_of).reshape((-1,) + (1,) * (len(extent) - position - 1))

    factor_of = one(*split[0])
    for cut in split[1:]:
        factor_of = factor_of * one(*cut)
    return factor_of


def centred(rng, shape, scale, reach, cuts=(), held_as=jnp.bfloat16):
    array = scale * jax.random.normal(rng, shape, jnp.float32)
    if cuts:
        array = array * shard_levels(rng, shape, cuts, -0.22, 0.18)
    return jnp.clip(array, -reach, reach).astype(held_as)


def setup_inputs(seed: int = 0) -> dict:
    arg_keys = jax.random.split(jax.random.key(seed), 9)
    state = centred(arg_keys[0], (MEMBERS, LEVELS, CELLS), 1.0, 6.0, ((0, 8), (2, 4)), jnp.float32)
    adjacent_columns = draw_adjacent_columns(jax.random.fold_in(arg_keys[8], 71), 0)
    adjacent_rates = jnp.clip(0.02 + 0.14 * jax.random.uniform(arg_keys[2], (6, CELLS), jnp.float32) ** shard_levels(arg_keys[2], (6, CELLS), ((1, 4),), -0.2, 0.2), 0.02, 0.16)
    amplification_speed = jnp.clip(jnp.exp(math.log(0.5) - 2.3025851 * jax.random.uniform(arg_keys[3], (CELLS,), jnp.float32) ** shard_levels(arg_keys[3], (CELLS,), ((0, 4),), -0.2, 0.2)), 0.05, 0.5)
    obs_patch = draw_obs_patch(jax.random.fold_in(arg_keys[8], 71), 0)
    obs_row = set_ends(jax.random.randint(arg_keys[5], (OBS_TOTAL,), 0, LEVELS * PATCH_CELLS), jax.random.fold_in(arg_keys[5], 1), 0, (LEVELS * PATCH_CELLS) - 1).astype(jnp.int32)
    obs_value = centred(arg_keys[6], (OBS_TOTAL,), 1.0, 6.0, ((0, 32),), jnp.float32)
    obs_error = jnp.clip(jnp.exp(math.log(2.0) - 1.3862944 * jax.random.uniform(arg_keys[7], (OBS_TOTAL,), jnp.float32) ** shard_levels(arg_keys[7], (OBS_TOTAL,), ((0, 32),), -0.2, 0.2)), 0.5, 2.0)
    return dict(state=state, adjacent_columns=adjacent_columns, adjacent_rates=adjacent_rates, amplification_speed=amplification_speed, obs_patch=obs_patch, obs_row=obs_row, obs_value=obs_value, obs_error=obs_error)


def propagate_prediction(model_variable_array, adjacent_columns, adjacent_rates, amplification_speed):
    summed = jnp.zeros_like(model_variable_array)
    for neighbour in range(6):
        summed = summed + adjacent_rates[neighbour] * (jnp.take(model_variable_array, adjacent_columns[neighbour], axis=2) - model_variable_array)
    blended = model_variable_array + summed
    return blended + amplification_speed * jnp.tanh(blended)

def analyse(ensemble_realizations, row_index, values, weight_matrix):
    ensemble = ensemble_realizations.shape[0]
    average = lax.optimization_barrier(jnp.mean(ensemble_realizations, axis=0))
    anomaly = ensemble_realizations - average[None, :]
    observed = jnp.take(anomaly, row_index, axis=1)
    innovation = values - jnp.take(average, row_index)
    rooted = jnp.sqrt(weight_matrix)
    spread = math.sqrt(ensemble - 1.0)
    scaled = observed * rooted[None, :] / spread
    identity = jnp.eye(ensemble, dtype=jnp.float32)
    system = identity + jnp.dot(scaled, scaled.T, precision=lax.Precision.HIGHEST)
    norm_fro = jnp.sqrt(jnp.sum(system * system))
    iterate = system / norm_fro
    inverse_root = identity
    for sweep in range(NS_ITERS):
        factor = 1.5 * identity - 0.5 * jnp.dot(inverse_root, iterate, precision=lax.Precision.HIGHEST)
        iterate = jnp.dot(iterate, factor, precision=lax.Precision.HIGHEST)
        inverse_root = jnp.dot(factor, inverse_root, precision=lax.Precision.HIGHEST)
    forcing_term = jnp.dot(scaled, rooted * innovation, precision=lax.Precision.HIGHEST) / spread
    inner_shift = jnp.dot(inverse_root, forcing_term, precision=lax.Precision.HIGHEST)
    mean_shift = jnp.dot(inverse_root, inner_shift, precision=lax.Precision.HIGHEST) / norm_fro
    transform = inverse_root / jnp.sqrt(norm_fro) + mean_shift[:, None]
    updated = average[None, :] + jnp.dot(transform.T, anomaly, precision=lax.Precision.HIGHEST)
    return updated.astype(jnp.bfloat16)

def reference(state, adjacent_columns, adjacent_rates, amplification_speed, obs_patch, obs_row, obs_value, obs_error):
    model_variable_array = state
    for section_index in range(STEPS):
        model_variable_array = propagate_prediction(model_variable_array, adjacent_columns, adjacent_rates, amplification_speed)
    rounded = model_variable_array.astype(jnp.bfloat16)
    widened = lax.optimization_barrier(rounded).astype(jnp.float32)
    grouped = widened.reshape(MEMBERS, LEVELS, PATCHES, PATCH_CELLS).transpose(2, 0, 1, 3)
    grouped = grouped.reshape(PATCHES, MEMBERS, LEVELS * PATCH_CELLS)
    is_live = obs_patch >= 0
    sort_key = jnp.where(is_live, obs_patch, PATCHES).astype(jnp.int32)
    ordering = jnp.argsort(sort_key, stable=True)
    sorted_key = sort_key[ordering]
    starts = jnp.searchsorted(sorted_key, jnp.arange(PATCHES, dtype=jnp.int32)).astype(jnp.int32)
    ranking = jnp.arange(OBS_TOTAL, dtype=jnp.int32) - starts[jnp.minimum(sorted_key, PATCHES - 1)]
    row_grid = jnp.zeros((PATCHES, PATCH_OBS), jnp.int32).at[sorted_key, ranking].set(obs_row[ordering].astype(jnp.int32), mode='drop')
    value_grid = jnp.zeros((PATCHES, PATCH_OBS), jnp.float32).at[sorted_key, ranking].set(obs_value[ordering], mode='drop')
    weight_all = 1.0 / (obs_error * obs_error)
    analysis_coefficient_array = jnp.zeros((PATCHES, PATCH_OBS), jnp.float32).at[sorted_key, ranking].set(weight_all[ordering], mode='drop')
    analysed = lax.map(lambda bundle: analyse(bundle[0], bundle[1], bundle[2], bundle[3]), (grouped, row_grid, value_grid, analysis_coefficient_array))
    analysed = analysed.reshape(PATCHES, MEMBERS, LEVELS, PATCH_CELLS).transpose(1, 2, 0, 3)
    return analysed.reshape(MEMBERS, LEVELS, CELLS)
```

```python
import functools
import math

import jax
import jax.numpy as jnp
from jax import lax
from jax.experimental import pallas as pl
from jax.experimental.pallas import tpu as pltpu
from jax.sharding import PartitionSpec as P

PATCH_CELLS = 128
RIM = 256
STEPS = 3
NS_ITERS = 6
CHUNKS = 2
F32 = jnp.float32
BF16 = jnp.bfloat16
NN = ((1,), (0,))
NT = ((1,), (1,))
TN = ((0,), (0,))


def dot(a, b, dims=NN):
    return lax.dot_general(a, b, (dims, ((), ())), preferred_element_type=F32)


def halves(a):
    high = a.astype(BF16)
    return high, (a - high.astype(F32)).astype(BF16)


def dot_pair(a, b, dims=NN):
    return dot(a[0], b[0], dims) + (dot(a[0], b[1], dims) + dot(a[1], b[0], dims))


def iota(shape, axis):
    return lax.broadcasted_iota(jnp.int32, shape, axis)


def kernel(
    groups, regions, slots,
    state, adjacent, rates, speed, obs_patch, obs_row, obs_value, obs_error,
    out,
    field, pad, mats, final, ensemble, message, relay, got, result, returned, merged,
    halo_send, halo_recv, first_send, first_recv, second_send, second_recv,
    spread_send, spread_recv, back_send, back_recv,
):
    me = lax.axis_index("member")
    here = lax.axis_index("region")
    right = lax.rem(here + 1, regions)
    left = lax.rem(here + regions - 1, regions)
    members, levels, length = state.shape
    rows = members * levels
    members_all = members * groups
    cells_all = length * regions
    blocks = length // RIM

    barrier = pltpu.get_barrier_semaphore()
    for step in range(1, groups):
        pl.semaphore_signal(barrier, inc=1, device_id={"member": lax.rem(me + step, groups)})
    for step in range(1, regions):
        pl.semaphore_signal(barrier, inc=1, device_id={"region": lax.rem(here + step, regions)})

    for level in range(levels):
        value = state[:, level, :]
        part = pl.ds(level * members, members)
        field[part, :] = value
        pad[0, part, RIM:RIM + length] = value.astype(BF16)

    pl.semaphore_wait(barrier, groups + regions - 2)

    height = rows // CHUNKS

    def halo(step, chunk):
        part = pl.ds(chunk * height, height)
        to_left = pltpu.make_async_remote_copy(
            src_ref=pad.at[step, part, pl.ds(RIM, RIM)],
            dst_ref=pad.at[step, part, pl.ds(RIM + length, RIM)],
            send_sem=halo_send.at[step, chunk, 0],
            recv_sem=halo_recv.at[step, chunk, 1],
            device_id={"region": left},
        )
        to_right = pltpu.make_async_remote_copy(
            src_ref=pad.at[step, part, pl.ds(length, RIM)],
            dst_ref=pad.at[step, part, pl.ds(0, RIM)],
            send_sem=halo_send.at[step, chunk, 1],
            recv_sem=halo_recv.at[step, chunk, 0],
            device_id={"region": right},
        )
        return to_left, to_right

    for chunk in range(CHUNKS):
        for copy in halo(0, chunk):
            copy.start()

    def first(target, source):
        return pltpu.make_async_remote_copy(
            src_ref=message.at[target], dst_ref=relay.at[source],
            send_sem=first_send.at[target], recv_sem=first_recv.at[source],
            device_id={"region": target},
        )

    def second(target, source):
        return pltpu.make_async_remote_copy(
            src_ref=relay.at[:, pl.ds(target * slots, slots), :], dst_ref=got.at[source],
            send_sem=second_send.at[target], recv_sem=second_recv.at[source],
            device_id={"member": target},
        )

    devices = groups * regions
    patch = obs_patch[...]
    count = patch.shape[1]
    live = patch >= 0
    one_hot = (iota((devices, count), 0) == patch).astype(F32)
    upper = (iota((count, count), 0) <= iota((count, count), 1)).astype(F32)
    counts = dot(one_hot.astype(BF16), upper.astype(BF16))
    rank = jnp.sum(counts * one_hot, axis=0, keepdims=True) - 1.0
    spot = jnp.where(live, patch * slots + rank.astype(jnp.int32), -1)
    error = obs_error[...]
    payload = jnp.concatenate(
        [
            (obs_row[...] + 1).astype(F32), obs_value[...], 1.0 / (error * error),
            jnp.zeros((125, count), F32),
        ],
        axis=0,
    )
    place = (iota((devices * slots, count), 0) == spot).astype(F32).astype(BF16)
    high = payload.astype(BF16)
    rest = payload - high.astype(F32)
    middle, low = halves(rest)
    bundle = dot(place, high, NT) + dot(place, middle, NT) + dot(place, low, NT)
    message[...] = bundle.reshape(regions, groups * slots, 128)
    for region in range(regions):
        @pl.when(here != region)
        def _():
            first(region, here).start()
    relay[here] = message[here]

    cell = here * length + iota((1, length), 1)
    offset = adjacent[...] - cell
    offset = jnp.where(offset > cells_all // 2, offset - cells_all, offset)
    offset = jnp.where(offset < -(cells_all // 2), offset + cells_all, offset)
    source = offset + RIM + lax.rem(iota((1, length), 1), RIM)
    rate = rates[...]
    keep = 1.0 - jnp.sum(rate, axis=0, keepdims=True)
    pace = speed[...]
    window = 3 * RIM
    slab = 128
    for block in range(blocks):
        cut = slice(block * RIM, (block + 1) * RIM)
        local, weight = source[:, cut], rate[:, cut]

        def build(index, carry):
            start = pl.multiple_of(index * slab, slab)
            row = iota((slab, RIM), 0) + start
            total = jnp.zeros((slab, RIM), F32)
            for k in range(6):
                total = total + jnp.where(row == local[k:k + 1], weight[k:k + 1], 0.0)
            mats[block, pl.ds(start, slab), :] = total.astype(BF16)
            return carry

        lax.fori_loop(0, window // slab, build, 0)

    for region in range(regions):
        @pl.when(here != region)
        def _():
            first(here, region).wait_recv()
    for member in range(groups):
        @pl.when(me != member)
        def _():
            second(member, me).start()
    got[me] = relay[:, pl.ds(pl.multiple_of(me * slots, slots), slots), :]

    def advance(step, block, start, size):
        part = pl.ds(start, size)
        cut = pl.ds(block * RIM, RIM)
        share = slice(block * RIM, (block + 1) * RIM)
        taken = pad[step, part, block * RIM:block * RIM + window]
        blended = field[part, cut] * keep[:, share] + dot(taken, mats[block])
        new = blended + pace[:, share] * jnp.tanh(blended)
        if step < STEPS - 1:
            field[part, cut] = new
            pad[step + 1, part, pl.ds(RIM + block * RIM, RIM)] = new.astype(BF16)
        else:
            rounded = new.astype(BF16)
            lots = RIM // PATCH_CELLS
            for lot in range(lots):
                piece = rounded[:, lot * PATCH_CELLS:(lot + 1) * PATCH_CELLS]
                final[block * lots + lot, start // members:(start + size) // members] = (
                    piece.reshape(size // members, members, PATCH_CELLS)
                )

    def spread(target, origin):
        return pltpu.make_async_remote_copy(
            src_ref=final.at[target],
            dst_ref=ensemble.at[:, pl.ds(pl.multiple_of(origin * members, members), members), :],
            send_sem=spread_send.at[target], recv_sem=spread_recv.at[origin],
            device_id={"member": target},
        )

    def hand_out(targets):
        for target in targets:
            @pl.when(me != target)
            def _():
                spread(target, me).start()

    lots = RIM // PATCH_CELLS
    for step in range(STEPS):
        for block in range(1, blocks - 1):
            advance(step, block, 0, rows)
        if step == STEPS - 1:
            hand_out(range(lots, groups - lots))
        for chunk in range(CHUNKS):
            _, to_right = halo(step, chunk)
            to_right.wait_recv()
            advance(step, 0, chunk * height, height)
            if step < STEPS - 1:
                halo(step + 1, chunk)[0].start()
            to_left, _ = halo(step, chunk)
            to_left.wait_recv()
            advance(step, blocks - 1, chunk * height, height)
            if step < STEPS - 1:
                halo(step + 1, chunk)[1].start()
    hand_out(list(range(lots)) + list(range(groups - lots, groups)))
    ensemble[:, pl.ds(pl.multiple_of(me * members, members), members), :] = final[me]

    for member in range(groups):
        @pl.when(me != member)
        def _():
            second(me, member).wait_recv()
    span = levels * PATCH_CELLS
    seen = got[...].reshape(devices * slots, 128)
    location = seen[:, 0:1].astype(jnp.int32) - 1
    reading, weight = seen[:, 1:2], seen[:, 2:3]
    select = (iota((devices * slots, span), 1) == location).astype(F32).astype(BF16)
    rooted = jnp.sqrt(weight)
    divisor = math.sqrt(members_all - 1.0)

    for member in range(groups):
        @pl.when(me != member)
        def _():
            spread(me, member).wait_recv()
    whole = jnp.concatenate([ensemble[level] for level in range(levels)], axis=1)
    observed = dot(select, whole, NT)
    average_observed = jnp.sum(observed, axis=1, keepdims=True) * (1.0 / members_all)
    scaled = (observed - average_observed) * (rooted / divisor)
    innovation = rooted * (reading - average_observed)
    forcing = jnp.sum(scaled * innovation, axis=0, keepdims=True) / divisor
    identity = (
        iota((members_all, members_all), 0) == iota((members_all, members_all), 1)
    ).astype(F32)
    parts = halves(scaled)
    system = identity + dot_pair(parts, parts, TN)
    norm = jnp.sqrt(jnp.sum(system * system, keepdims=True))
    iterate = system / norm
    factor = 1.5 * identity - 0.5 * iterate
    factor_parts = halves(factor)
    iterate = dot_pair(halves(iterate), factor_parts)
    inverse = factor
    inverse_parts = factor_parts
    for sweep in range(1, NS_ITERS):
        iterate_parts = halves(iterate)
        factor = 1.5 * identity - 0.5 * dot_pair(inverse_parts, iterate_parts)
        factor_parts = halves(factor)
        if sweep < NS_ITERS - 1:
            iterate = dot_pair(iterate_parts, factor_parts)
        inverse = dot_pair(factor_parts, inverse_parts)
        inverse_parts = halves(inverse)
    inner = jnp.sum(inverse * forcing, axis=1, keepdims=True)
    shift = jnp.sum(inverse * inner, axis=0, keepdims=True) / norm
    transform = halves(inverse / jnp.sqrt(norm) + shift)

    wide = whole.astype(F32)
    average = jnp.sum(wide, axis=0, keepdims=True) * (1.0 / members_all)
    anomaly = halves(wide - average)
    updated = (average + dot_pair(transform, anomaly)).astype(BF16)
    for level in range(levels):
        result[level] = updated[:, level * PATCH_CELLS:(level + 1) * PATCH_CELLS]

    def back(target, origin):
        return pltpu.make_async_remote_copy(
            src_ref=result.at[:, pl.ds(pl.multiple_of(target * members, members), members), :],
            dst_ref=returned.at[origin],
            send_sem=back_send.at[target], recv_sem=back_recv.at[origin],
            device_id={"member": target},
        )

    for target in range(groups):
        @pl.when(me != target)
        def _():
            back(target, me).start()
    returned[me] = result[:, pl.ds(pl.multiple_of(me * members, members), members), :]

    for step in range(STEPS):
        for chunk in range(CHUNKS):
            for copy in halo(step, chunk):
                copy.wait_send()
    for region in range(regions):
        @pl.when(here != region)
        def _():
            first(region, here).wait_send()
    for member in range(groups):
        @pl.when(me != member)
        def _():
            second(member, me).wait_send()
            spread(member, me).wait_send()
            back(me, member).wait_recv()
    for origin in range(groups):
        for level in range(levels):
            merged[:, level, origin * PATCH_CELLS:(origin + 1) * PATCH_CELLS] = (
                returned[origin, level].astype(F32)
            )
    out[...] = merged[...].astype(BF16)
    for member in range(groups):
        @pl.when(me != member)
        def _():
            back(member, me).wait_send()


def on_device(
    state, adjacent_columns, adjacent_rates, amplification_speed,
    obs_patch, obs_row, obs_value, obs_error,
):
    members, levels, length = state.shape
    groups = lax.axis_size("member")
    regions = lax.axis_size("region")
    rows = members * levels
    members_all = members * groups
    count = obs_patch.shape[0]
    slots = -(-count // (groups * regions) // 8) * 8
    dma = pltpu.SemaphoreType.DMA
    vmem = pl.BlockSpec(memory_space=pltpu.VMEM)
    return pl.pallas_call(
        functools.partial(kernel, groups, regions, slots),
        out_shape=jax.ShapeDtypeStruct((members, levels, length), BF16),
        in_specs=[vmem] * 8,
        out_specs=vmem,
        scratch_shapes=[
            pltpu.VMEM((rows, length), F32),
            pltpu.VMEM((STEPS, rows, length + 2 * RIM), BF16),
            pltpu.VMEM((length // RIM, 3 * RIM, RIM), BF16),
            pltpu.VMEM((groups, levels, members, PATCH_CELLS), BF16),
            pltpu.VMEM((levels, members_all, PATCH_CELLS), BF16),
            pltpu.VMEM((regions, groups * slots, 128), F32),
            pltpu.VMEM((regions, groups * slots, 128), F32),
            pltpu.VMEM((groups, regions, slots, 128), F32),
            pltpu.VMEM((levels, members_all, PATCH_CELLS), BF16),
            pltpu.VMEM((groups, levels, members, PATCH_CELLS), BF16),
            pltpu.VMEM((members, levels, length), F32),
            dma((STEPS, CHUNKS, 2)), dma((STEPS, CHUNKS, 2)),
            dma((regions,)), dma((regions,)),
            dma((groups,)), dma((groups,)),
            dma((groups,)), dma((groups,)),
            dma((groups,)), dma((groups,)),
        ],
        compiler_params=pltpu.CompilerParams(
            collective_id=0, has_side_effects=True, vmem_limit_bytes=56 * 1024 * 1024
        ),
    )(
        state, adjacent_columns, adjacent_rates, amplification_speed[None, :],
        obs_patch[None, :], obs_row[None, :], obs_value[None, :], obs_error[None, :],
    )


def solution(mesh):
    return jax.shard_map(
        on_device,
        mesh=mesh,
        in_specs=(
            P("member", None, "region"),
            P(None, "region"),
            P(None, "region"),
            P("region"),
            P(("member", "region")),
            P(("member", "region")),
            P(("member", "region")),
            P(("member", "region")),
        ),
        out_specs=P("member", None, "region"),
        check_vma=False,
    )
```

```python
import functools
import math

import jax
import jax.numpy as jnp
from jax import lax
from jax.experimental import pallas as pl
from jax.experimental.pallas import tpu as pltpu
from jax.sharding import PartitionSpec as P

PATCH_CELLS = 128
RIM = 256
STEPS = 3
NS_ITERS = 6
CHUNKS = 4
PARTS = 1
F32 = jnp.float32
BF16 = jnp.bfloat16
NN = ((1,), (0,))
NT = ((1,), (1,))
TN = ((0,), (0,))


def dot(a, b, dims=NN):
    return lax.dot_general(a, b, (dims, ((), ())), preferred_element_type=F32)


def halves(a):
    high = a.astype(BF16)
    return high, (a - high.astype(F32)).astype(BF16)


def dot_pair(a, b, dims=NN):
    return dot(a[0], b[0], dims) + (dot(a[0], b[1], dims) + dot(a[1], b[0], dims))


def iota(shape, axis):
    return lax.broadcasted_iota(jnp.int32, shape, axis)


def kernel(
    groups, regions, slots,
    state, adjacent, rates, speed, obs_patch, obs_row, obs_value, obs_error,
    out,
    field, pad, mats, final, ensemble, message, relay, dense, got, result, returned, merged,
    halo_send, halo_recv, first_send, first_recv, second_send, second_recv,
    spread_send, spread_recv, back_send, back_recv,
):
    me = lax.axis_index("member")
    here = lax.axis_index("region")
    right = lax.rem(here + 1, regions)
    left = lax.rem(here + regions - 1, regions)
    members, levels, length = state.shape
    rows = members * levels
    members_all = members * groups
    cells_all = length * regions
    blocks = length // RIM

    barrier = pltpu.get_barrier_semaphore()
    for step in range(1, groups):
        pl.semaphore_signal(barrier, inc=1, device_id={"member": lax.rem(me + step, groups)})
    for step in range(1, regions):
        pl.semaphore_signal(barrier, inc=1, device_id={"region": lax.rem(here + step, regions)})

    def load(block):
        for level in range(levels):
            value = state[:, level, block * RIM:(block + 1) * RIM]
            part = pl.ds(level * members, members)
            field[part, block * RIM:(block + 1) * RIM] = value
            pad[0, part, (block + 1) * RIM:(block + 2) * RIM] = value.astype(BF16)

    load(0)
    load(blocks - 1)
    pl.semaphore_wait(barrier, groups + regions - 2)

    height = rows // CHUNKS

    def halo(step, chunk, side):
        part = pl.ds(chunk * height, height)
        if side == 0:
            return pltpu.make_async_remote_copy(
                src_ref=pad.at[step, part, pl.ds(RIM, RIM)],
                dst_ref=pad.at[step, part, pl.ds(RIM + length, RIM)],
                send_sem=halo_send.at[step, chunk, 0],
                recv_sem=halo_recv.at[step, chunk, 1],
                device_id={"region": left},
            )
        return pltpu.make_async_remote_copy(
            src_ref=pad.at[step, part, pl.ds(length, RIM)],
            dst_ref=pad.at[step, part, pl.ds(0, RIM)],
            send_sem=halo_send.at[step, chunk, 1],
            recv_sem=halo_recv.at[step, chunk, 0],
            device_id={"region": right},
        )

    for chunk in range(CHUNKS):
        for side in range(2):
            halo(0, chunk, side).start()
    for block in range(1, blocks - 1):
        load(block)

    def first(target, origin):
        return pltpu.make_async_remote_copy(
            src_ref=message.at[target], dst_ref=relay.at[origin],
            send_sem=first_send.at[target], recv_sem=first_recv.at[origin],
            device_id={"member": target},
        )

    def second(target, origin):
        return pltpu.make_async_remote_copy(
            src_ref=dense.at[target], dst_ref=got.at[origin],
            send_sem=second_send.at[target], recv_sem=second_recv.at[origin],
            device_id={"region": target},
        )

    devices = groups * regions
    patch = obs_patch[...]
    count = patch.shape[1]
    live = patch >= 0
    one_hot = (iota((devices, count), 0) == patch).astype(F32)
    upper = (iota((count, count), 0) <= iota((count, count), 1)).astype(F32)
    counts = dot(one_hot.astype(BF16), upper.astype(BF16))
    rank = jnp.sum(counts * one_hot, axis=0, keepdims=True) - 1.0
    desk = lax.rem(patch, groups) * regions + patch // groups
    spot = jnp.where(live, desk * slots + rank.astype(jnp.int32), -1)
    error = obs_error[...]
    payload = jnp.concatenate(
        [
            (obs_row[...] + 1).astype(F32), obs_value[...], 1.0 / (error * error),
            jnp.zeros((125, count), F32),
        ],
        axis=0,
    )
    place = (iota((devices * slots, count), 0) == spot).astype(F32).astype(BF16)
    high = payload.astype(BF16)
    rest = payload - high.astype(F32)
    middle, low = halves(rest)
    bundle = dot(place, high, NT) + dot(place, middle, NT) + dot(place, low, NT)
    message[...] = bundle.reshape(groups, regions, slots, 128)
    for member in range(groups):
        @pl.when(me != member)
        def _():
            first(member, me).start()
    relay[me] = message[me]

    cell = here * length + iota((1, length), 1)
    offset = adjacent[...] - cell
    offset = jnp.where(offset > cells_all // 2, offset - cells_all, offset)
    offset = jnp.where(offset < -(cells_all // 2), offset + cells_all, offset)
    source = offset + RIM + lax.rem(iota((1, length), 1), RIM)
    rate = rates[...]
    keep = 1.0 - jnp.sum(rate, axis=0, keepdims=True)
    pace = speed[...]
    window = 3 * RIM
    slab = 128
    for block in range(blocks):
        cut = slice(block * RIM, (block + 1) * RIM)
        local, weight = source[:, cut], rate[:, cut]

        def build(index, carry):
            start = pl.multiple_of(index * slab, slab)
            row = iota((slab, RIM), 0) + start
            total = jnp.zeros((slab, RIM), F32)
            for k in range(6):
                total = total + jnp.where(row == local[k:k + 1], weight[k:k + 1], 0.0)
            mats[block, pl.ds(start, slab), :] = total.astype(BF16)
            return carry

        lax.fori_loop(0, window // slab, build, 0)

    for member in range(groups):
        @pl.when(me != member)
        def _():
            first(me, member).wait_recv()
    used = groups * slots
    lanes = dense.shape[2]
    for region in range(regions):
        block = relay[:, region].reshape(used, 128)
        if lanes > used:
            block = jnp.concatenate([block, jnp.zeros((lanes - used, 128), F32)], axis=0)
        dense[region] = block.T[:8]
    for region in range(regions):
        @pl.when(here != region)
        def _():
            second(region, here).start()
    got[here] = dense[here]

    def advance(step, block, start, size):
        part = pl.ds(start, size)
        cut = pl.ds(block * RIM, RIM)
        share = slice(block * RIM, (block + 1) * RIM)
        taken = pad[step, part, block * RIM:block * RIM + window]
        blended = field[part, cut] * keep[:, share] + dot(taken, mats[block])
        new = blended + pace[:, share] * jnp.tanh(blended)
        if step < STEPS - 1:
            field[part, cut] = new
            pad[step + 1, part, pl.ds(RIM + block * RIM, RIM)] = new.astype(BF16)
        else:
            rounded = new.astype(BF16)
            lots = RIM // PATCH_CELLS
            for lot in range(lots):
                piece = rounded[:, lot * PATCH_CELLS:(lot + 1) * PATCH_CELLS]
                final[block * lots + lot, start // members:(start + size) // members] = (
                    piece.reshape(size // members, members, PATCH_CELLS)
                )

    deep = levels // CHUNKS

    def spread(target, origin, chunk):
        part = pl.ds(chunk * deep, deep)
        place = pl.ds(pl.multiple_of(origin * members, members), members)
        return pltpu.make_async_remote_copy(
            src_ref=final.at[target, part],
            dst_ref=ensemble.at[part, place, :],
            send_sem=spread_send.at[target, chunk], recv_sem=spread_recv.at[origin, chunk],
            device_id={"member": target},
        )

    def hand_out(targets, chunk):
        for target in targets:
            @pl.when(me != target)
            def _():
                spread(target, me, chunk).start()

    lots = RIM // PATCH_CELLS
    for step in range(STEPS):
        for block in range(1, blocks - 1):
            advance(step, block, 0, rows)
        if step == STEPS - 1:
            for chunk in range(CHUNKS):
                hand_out(range(lots, groups - lots), chunk)
        for chunk in range(CHUNKS):
            halo(step, chunk, 1).wait_recv()
            advance(step, 0, chunk * height, height)
            if step < STEPS - 1:
                halo(step + 1, chunk, 0).start()
            else:
                hand_out(range(lots), chunk)
            halo(step, chunk, 0).wait_recv()
            advance(step, blocks - 1, chunk * height, height)
            if step < STEPS - 1:
                halo(step + 1, chunk, 1).start()
            else:
                hand_out(range(groups - lots, groups), chunk)
    ensemble[:, pl.ds(pl.multiple_of(me * members, members), members), :] = final[me]

    for region in range(regions):
        @pl.when(here != region)
        def _():
            second(here, region).wait_recv()
    span = levels * PATCH_CELLS
    seen = jnp.concatenate(
        [
            jnp.concatenate([got[region], jnp.zeros((120, lanes), F32)], axis=0).T[:used]
            for region in range(regions)
        ],
        axis=0,
    )
    location = seen[:, 0:1].astype(jnp.int32) - 1
    reading, weight = seen[:, 1:2], seen[:, 2:3]
    select = (iota((devices * slots, span), 1) == location).astype(F32).astype(BF16)
    rooted = jnp.sqrt(weight)
    divisor = math.sqrt(members_all - 1.0)

    for member in range(groups):
        @pl.when(me != member)
        def _():
            for chunk in range(CHUNKS):
                spread(me, member, chunk).wait_recv()
    whole = jnp.concatenate([ensemble[level] for level in range(levels)], axis=1)
    observed = dot(select, whole, NT)
    average_observed = jnp.sum(observed, axis=1, keepdims=True) * (1.0 / members_all)
    scaled = (observed - average_observed) * (rooted / divisor)
    innovation = rooted * (reading - average_observed)
    forcing = jnp.sum(scaled * innovation, axis=0, keepdims=True) / divisor
    identity = (
        iota((members_all, members_all), 0) == iota((members_all, members_all), 1)
    ).astype(F32)
    parts = halves(scaled)
    system = identity + dot_pair(parts, parts, TN)
    norm = jnp.sqrt(jnp.sum(system * system, keepdims=True))
    iterate = system / norm
    factor = 1.5 * identity - 0.5 * iterate
    factor_parts = halves(factor)
    iterate = dot_pair(halves(iterate), factor_parts)
    inverse = factor
    inverse_parts = factor_parts
    for sweep in range(1, NS_ITERS):
        iterate_parts = halves(iterate)
        factor = 1.5 * identity - 0.5 * dot_pair(inverse_parts, iterate_parts)
        factor_parts = halves(factor)
        if sweep < NS_ITERS - 1:
            iterate = dot_pair(iterate_parts, factor_parts)
        inverse = dot_pair(factor_parts, inverse_parts)
        inverse_parts = halves(inverse)
    inner = jnp.sum(inverse * forcing, axis=1, keepdims=True)
    shift = jnp.sum(inverse * inner, axis=0, keepdims=True) / norm
    transform = halves(inverse / jnp.sqrt(norm) + shift)

    wide = whole.astype(F32)
    average = jnp.sum(wide, axis=0, keepdims=True) * (1.0 / members_all)
    anomaly = halves(wide - average)
    slim = levels // PARTS

    def back(target, origin, part):
        depth = pl.ds(part * slim, slim)
        place = pl.ds(pl.multiple_of(target * members, members), members)
        return pltpu.make_async_remote_copy(
            src_ref=result.at[depth, place, :],
            dst_ref=returned.at[origin, depth],
            send_sem=back_send.at[target, part], recv_sem=back_recv.at[origin, part],
            device_id={"member": target},
        )

    for part in range(PARTS):
        cut = slice(part * slim * PATCH_CELLS, (part + 1) * slim * PATCH_CELLS)
        taken = anomaly[0][:, cut], anomaly[1][:, cut]
        updated = (average[:, cut] + dot_pair(transform, taken)).astype(BF16)
        for level in range(slim):
            result[part * slim + level] = updated[:, level * PATCH_CELLS:(level + 1) * PATCH_CELLS]
        for step in range(1, groups):
            back(lax.rem(me + step, groups), me, part).start()
    returned[me] = result[:, pl.ds(pl.multiple_of(me * members, members), members), :]

    for step in range(STEPS):
        for chunk in range(CHUNKS):
            for side in range(2):
                halo(step, chunk, side).wait_send()
    for region in range(regions):
        @pl.when(here != region)
        def _():
            second(region, here).wait_send()
    for member in range(groups):
        @pl.when(me != member)
        def _():
            first(member, me).wait_send()
            for chunk in range(CHUNKS):
                spread(member, me, chunk).wait_send()
    for origin in range(groups):
        @pl.when(me != origin)
        def _():
            for part in range(PARTS):
                back(me, origin, part).wait_recv()
        for level in range(levels):
            merged[:, level, origin * PATCH_CELLS:(origin + 1) * PATCH_CELLS] = (
                returned[origin, level].astype(F32)
            )
    out[...] = merged[...].astype(BF16)
    for member in range(groups):
        @pl.when(me != member)
        def _():
            for part in range(PARTS):
                back(member, me, part).wait_send()


def on_device(
    state, adjacent_columns, adjacent_rates, amplification_speed,
    obs_patch, obs_row, obs_value, obs_error,
):
    members, levels, length = state.shape
    groups = lax.axis_size("member")
    regions = lax.axis_size("region")
    rows = members * levels
    members_all = members * groups
    count = obs_patch.shape[0]
    slots = -(-count // (groups * regions) // 8) * 8
    dma = pltpu.SemaphoreType.DMA
    vmem = pl.BlockSpec(memory_space=pltpu.VMEM)
    return pl.pallas_call(
        functools.partial(kernel, groups, regions, slots),
        out_shape=jax.ShapeDtypeStruct((members, levels, length), BF16),
        in_specs=[vmem] * 8,
        out_specs=vmem,
        scratch_shapes=[
            pltpu.VMEM((rows, length), F32),
            pltpu.VMEM((STEPS, rows, length + 2 * RIM), BF16),
            pltpu.VMEM((length // RIM, 3 * RIM, RIM), BF16),
            pltpu.VMEM((groups, levels, members, PATCH_CELLS), BF16),
            pltpu.VMEM((levels, members_all, PATCH_CELLS), BF16),
            pltpu.VMEM((groups, regions, slots, 128), F32),
            pltpu.VMEM((groups, regions, slots, 128), F32),
            pltpu.VMEM((regions, 8, -(-groups * slots // 128) * 128), F32),
            pltpu.VMEM((regions, 8, -(-groups * slots // 128) * 128), F32),
            pltpu.VMEM((levels, members_all, PATCH_CELLS), BF16),
            pltpu.VMEM((groups, levels, members, PATCH_CELLS), BF16),
            pltpu.VMEM((members, levels, length), F32),
            dma((STEPS, CHUNKS, 2)), dma((STEPS, CHUNKS, 2)),
            dma((groups,)), dma((groups,)),
            dma((regions,)), dma((regions,)),
            dma((groups, CHUNKS)), dma((groups, CHUNKS)),
            dma((groups, PARTS)), dma((groups, PARTS)),
        ],
        compiler_params=pltpu.CompilerParams(
            collective_id=0, has_side_effects=True, vmem_limit_bytes=56 * 1024 * 1024
        ),
    )(
        state, adjacent_columns, adjacent_rates, amplification_speed[None, :],
        obs_patch[None, :], obs_row[None, :], obs_value[None, :], obs_error[None, :],
    )


def solution(mesh):
    return jax.shard_map(
        on_device,
        mesh=mesh,
        in_specs=(
            P("member", None, "region"),
            P(None, "region"),
            P(None, "region"),
            P("region"),
            P(("member", "region")),
            P(("member", "region")),
            P(("member", "region")),
            P(("member", "region")),
        ),
        out_specs=P("member", None, "region"),
        check_vma=False,
    )
```

```python
import functools
import math

import jax
import jax.numpy as jnp
from jax import lax
from jax.experimental import pallas as pl
from jax.experimental.pallas import tpu as pltpu
from jax.sharding import PartitionSpec as P

PATCH_CELLS = 128
RIM = 256
STEPS = 3
NS_ITERS = 6
CHUNKS = 4
PARTS = 1
F32 = jnp.float32
BF16 = jnp.bfloat16
NN = ((1,), (0,))
NT = ((1,), (1,))
TN = ((0,), (0,))


def dot(a, b, dims=NN):
    return lax.dot_general(a, b, (dims, ((), ())), preferred_element_type=F32)


def halves(a):
    high = a.astype(BF16)
    return high, (a - high.astype(F32)).astype(BF16)


def dot_pair(a, b, dims=NN):
    return dot(a[0], b[0], dims) + (dot(a[0], b[1], dims) + dot(a[1], b[0], dims))


def iota(shape, axis):
    return lax.broadcasted_iota(jnp.int32, shape, axis)


def kernel(
    groups, regions, slots,
    state, adjacent, rates, speed, obs_patch, obs_row, obs_value, obs_error,
    out,
    field, pad, mats, final, ensemble, message, relay, dense, got, result, returned, merged,
    halo_send, halo_recv, first_send, first_recv, second_send, second_recv,
    spread_send, spread_recv, back_send, back_recv, fetched,
):
    me = lax.axis_index("member")
    here = lax.axis_index("region")
    right = lax.rem(here + 1, regions)
    left = lax.rem(here + regions - 1, regions)
    members, levels, length = state.shape
    rows = members * levels
    members_all = members * groups
    cells_all = length * regions
    blocks = length // RIM

    barrier = pltpu.get_barrier_semaphore()
    for step in range(1, groups):
        pl.semaphore_signal(barrier, inc=1, device_id={"member": lax.rem(me + step, groups)})
    for step in range(1, regions):
        pl.semaphore_signal(barrier, inc=1, device_id={"region": lax.rem(here + step, regions)})

    def fetch(block):
        cut = pl.ds(block * RIM, RIM)
        return pltpu.make_async_copy(
            state.at[:, :, cut], merged.at[:, :, cut], fetched.at[block]
        )

    inner = list(range(1, blocks - 1))
    for block in [0, blocks - 1] + inner:
        fetch(block).start()

    def load(block):
        fetch(block).wait()
        for level in range(levels):
            value = merged[:, level, block * RIM:(block + 1) * RIM]
            part = pl.ds(level * members, members)
            field[part, block * RIM:(block + 1) * RIM] = value
            pad[0, part, (block + 1) * RIM:(block + 2) * RIM] = value.astype(BF16)

    load(0)
    load(blocks - 1)
    pl.semaphore_wait(barrier, groups + regions - 2)

    height = rows // CHUNKS

    def halo(step, chunk, side):
        part = pl.ds(chunk * height, height)
        if side == 0:
            return pltpu.make_async_remote_copy(
                src_ref=pad.at[step, part, pl.ds(RIM, RIM)],
                dst_ref=pad.at[step, part, pl.ds(RIM + length, RIM)],
                send_sem=halo_send.at[step, chunk, 0],
                recv_sem=halo_recv.at[step, chunk, 1],
                device_id={"region": left},
            )
        return pltpu.make_async_remote_copy(
            src_ref=pad.at[step, part, pl.ds(length, RIM)],
            dst_ref=pad.at[step, part, pl.ds(0, RIM)],
            send_sem=halo_send.at[step, chunk, 1],
            recv_sem=halo_recv.at[step, chunk, 0],
            device_id={"region": right},
        )

    for chunk in range(CHUNKS):
        for side in range(2):
            halo(0, chunk, side).start()
    for block in inner:
        load(block)

    def first(target, origin):
        return pltpu.make_async_remote_copy(
            src_ref=message.at[target], dst_ref=relay.at[origin],
            send_sem=first_send.at[target], recv_sem=first_recv.at[origin],
            device_id={"member": target},
        )

    def second(target, origin):
        return pltpu.make_async_remote_copy(
            src_ref=dense.at[target], dst_ref=got.at[origin],
            send_sem=second_send.at[target], recv_sem=second_recv.at[origin],
            device_id={"region": target},
        )

    devices = groups * regions
    patch = obs_patch[...]
    count = patch.shape[1]
    live = patch >= 0
    one_hot = (iota((devices, count), 0) == patch).astype(F32)
    upper = (iota((count, count), 0) <= iota((count, count), 1)).astype(F32)
    counts = dot(one_hot.astype(BF16), upper.astype(BF16))
    rank = jnp.sum(counts * one_hot, axis=0, keepdims=True) - 1.0
    desk = lax.rem(patch, groups) * regions + patch // groups
    spot = jnp.where(live, desk * slots + rank.astype(jnp.int32), -1)
    error = obs_error[...]
    payload = jnp.concatenate(
        [
            (obs_row[...] + 1).astype(F32), obs_value[...], 1.0 / (error * error),
            jnp.zeros((125, count), F32),
        ],
        axis=0,
    )
    place = (iota((devices * slots, count), 0) == spot).astype(F32).astype(BF16)
    high = payload.astype(BF16)
    rest = payload - high.astype(F32)
    middle, low = halves(rest)
    bundle = dot(place, high, NT) + dot(place, middle, NT) + dot(place, low, NT)
    message[...] = bundle.reshape(groups, regions, slots, 128)
    for member in range(groups):
        @pl.when(me != member)
        def _():
            first(member, me).start()
    relay[me] = message[me]

    cell = here * length + iota((1, length), 1)
    offset = adjacent[...] - cell
    offset = jnp.where(offset > cells_all // 2, offset - cells_all, offset)
    offset = jnp.where(offset < -(cells_all // 2), offset + cells_all, offset)
    source = offset + RIM + lax.rem(iota((1, length), 1), RIM)
    rate = rates[...]
    keep = 1.0 - jnp.sum(rate, axis=0, keepdims=True)
    pace = speed[...]
    window = 3 * RIM
    slab = 128
    for block in range(blocks):
        cut = slice(block * RIM, (block + 1) * RIM)
        local, weight = source[:, cut], rate[:, cut]

        def build(index, carry):
            start = pl.multiple_of(index * slab, slab)
            row = iota((slab, RIM), 0) + start
            total = jnp.zeros((slab, RIM), F32)
            for k in range(6):
                total = total + jnp.where(row == local[k:k + 1], weight[k:k + 1], 0.0)
            mats[block, pl.ds(start, slab), :] = total.astype(BF16)
            return carry

        lax.fori_loop(0, window // slab, build, 0)

    for member in range(groups):
        @pl.when(me != member)
        def _():
            first(me, member).wait_recv()
    used = groups * slots
    lanes = dense.shape[2]
    for region in range(regions):
        block = relay[:, region].reshape(used, 128)
        if lanes > used:
            block = jnp.concatenate([block, jnp.zeros((lanes - used, 128), F32)], axis=0)
        dense[region] = block.T[:8]
    for region in range(regions):
        @pl.when(here != region)
        def _():
            second(region, here).start()
    got[here] = dense[here]

    def advance(step, block, start, size):
        part = pl.ds(start, size)
        cut = pl.ds(block * RIM, RIM)
        share = slice(block * RIM, (block + 1) * RIM)
        taken = pad[step, part, block * RIM:block * RIM + window]
        blended = field[part, cut] * keep[:, share] + dot(taken, mats[block])
        new = blended + pace[:, share] * jnp.tanh(blended)
        if step < STEPS - 1:
            field[part, cut] = new
            pad[step + 1, part, pl.ds(RIM + block * RIM, RIM)] = new.astype(BF16)
        else:
            rounded = new.astype(BF16)
            lots = RIM // PATCH_CELLS
            for lot in range(lots):
                piece = rounded[:, lot * PATCH_CELLS:(lot + 1) * PATCH_CELLS]
                final[block * lots + lot, start // members:(start + size) // members] = (
                    piece.reshape(size // members, members, PATCH_CELLS)
                )

    deep = levels // CHUNKS

    def spread(target, origin, chunk):
        part = pl.ds(chunk * deep, deep)
        place = pl.ds(pl.multiple_of(origin * members, members), members)
        return pltpu.make_async_remote_copy(
            src_ref=final.at[target, part],
            dst_ref=ensemble.at[part, place, :],
            send_sem=spread_send.at[target, chunk], recv_sem=spread_recv.at[origin, chunk],
            device_id={"member": target},
        )

    def hand_out(targets, chunk):
        for target in targets:
            @pl.when(me != target)
            def _():
                spread(target, me, chunk).start()

    lots = RIM // PATCH_CELLS
    for step in range(STEPS):
        for block in range(1, blocks - 1):
            advance(step, block, 0, rows)
        if step == STEPS - 1:
            for chunk in range(CHUNKS):
                hand_out(range(lots, groups - lots), chunk)
        for chunk in range(CHUNKS):
            halo(step, chunk, 1).wait_recv()
            advance(step, 0, chunk * height, height)
            if step < STEPS - 1:
                halo(step + 1, chunk, 0).start()
            else:
                hand_out(range(lots), chunk)
            halo(step, chunk, 0).wait_recv()
            advance(step, blocks - 1, chunk * height, height)
            if step < STEPS - 1:
                halo(step + 1, chunk, 1).start()
            else:
                hand_out(range(groups - lots, groups), chunk)
    ensemble[:, pl.ds(pl.multiple_of(me * members, members), members), :] = final[me]

    for region in range(regions):
        @pl.when(here != region)
        def _():
            second(here, region).wait_recv()
    span = levels * PATCH_CELLS
    seen = jnp.concatenate(
        [
            jnp.concatenate([got[region], jnp.zeros((120, lanes), F32)], axis=0).T[:used]
            for region in range(regions)
        ],
        axis=0,
    )
    location = seen[:, 0:1].astype(jnp.int32) - 1
    reading, weight = seen[:, 1:2], seen[:, 2:3]
    select = (iota((devices * slots, span), 1) == location).astype(F32).astype(BF16)
    rooted = jnp.sqrt(weight)
    divisor = math.sqrt(members_all - 1.0)

    for member in range(groups):
        @pl.when(me != member)
        def _():
            for chunk in range(CHUNKS):
                spread(me, member, chunk).wait_recv()
    whole = jnp.concatenate([ensemble[level] for level in range(levels)], axis=1)
    observed = dot(select, whole, NT)
    average_observed = jnp.sum(observed, axis=1, keepdims=True) * (1.0 / members_all)
    scaled = (observed - average_observed) * (rooted / divisor)
    innovation = rooted * (reading - average_observed)
    forcing = jnp.sum(scaled * innovation, axis=0, keepdims=True) / divisor
    identity = (
        iota((members_all, members_all), 0) == iota((members_all, members_all), 1)
    ).astype(F32)
    parts = halves(scaled)
    system = identity + dot_pair(parts, parts, TN)
    norm = jnp.sqrt(jnp.sum(system * system, keepdims=True))
    iterate = system / norm
    factor = 1.5 * identity - 0.5 * iterate
    factor_parts = halves(factor)
    iterate = dot_pair(halves(iterate), factor_parts)
    inverse = factor
    inverse_parts = factor_parts
    for sweep in range(1, NS_ITERS):
        iterate_parts = halves(iterate)
        factor = 1.5 * identity - 0.5 * dot_pair(inverse_parts, iterate_parts)
        factor_parts = halves(factor)
        if sweep < NS_ITERS - 1:
            iterate = dot_pair(iterate_parts, factor_parts)
        inverse = dot_pair(factor_parts, inverse_parts)
        inverse_parts = halves(inverse)
    inner = jnp.sum(inverse * forcing, axis=1, keepdims=True)
    shift = jnp.sum(inverse * inner, axis=0, keepdims=True) / norm
    transform = halves(inverse / jnp.sqrt(norm) + shift)

    wide = whole.astype(F32)
    average = jnp.sum(wide, axis=0, keepdims=True) * (1.0 / members_all)
    anomaly = halves(wide - average)
    slim = levels // PARTS

    def back(target, origin, part):
        depth = pl.ds(part * slim, slim)
        place = pl.ds(pl.multiple_of(target * members, members), members)
        return pltpu.make_async_remote_copy(
            src_ref=result.at[depth, place, :],
            dst_ref=returned.at[origin, depth],
            send_sem=back_send.at[target, part], recv_sem=back_recv.at[origin, part],
            device_id={"member": target},
        )

    for part in range(PARTS):
        cut = slice(part * slim * PATCH_CELLS, (part + 1) * slim * PATCH_CELLS)
        taken = anomaly[0][:, cut], anomaly[1][:, cut]
        updated = (average[:, cut] + dot_pair(transform, taken)).astype(BF16)
        for level in range(slim):
            result[part * slim + level] = updated[:, level * PATCH_CELLS:(level + 1) * PATCH_CELLS]
        for step in range(1, groups):
            back(lax.rem(me + step, groups), me, part).start()
    returned[me] = result[:, pl.ds(pl.multiple_of(me * members, members), members), :]

    for step in range(STEPS):
        for chunk in range(CHUNKS):
            for side in range(2):
                halo(step, chunk, side).wait_send()
    for region in range(regions):
        @pl.when(here != region)
        def _():
            second(region, here).wait_send()
    for member in range(groups):
        @pl.when(me != member)
        def _():
            first(member, me).wait_send()
            for chunk in range(CHUNKS):
                spread(member, me, chunk).wait_send()
    for origin in range(groups):
        @pl.when(me != origin)
        def _():
            for part in range(PARTS):
                back(me, origin, part).wait_recv()
        for level in range(levels):
            merged[:, level, origin * PATCH_CELLS:(origin + 1) * PATCH_CELLS] = (
                returned[origin, level].astype(F32)
            )
    out[...] = merged[...].astype(BF16)
    for member in range(groups):
        @pl.when(me != member)
        def _():
            for part in range(PARTS):
                back(member, me, part).wait_send()


def on_device(
    state, adjacent_columns, adjacent_rates, amplification_speed,
    obs_patch, obs_row, obs_value, obs_error,
):
    members, levels, length = state.shape
    groups = lax.axis_size("member")
    regions = lax.axis_size("region")
    rows = members * levels
    members_all = members * groups
    count = obs_patch.shape[0]
    slots = -(-count // (groups * regions) // 8) * 8
    dma = pltpu.SemaphoreType.DMA
    vmem = pl.BlockSpec(memory_space=pltpu.VMEM)
    return pl.pallas_call(
        functools.partial(kernel, groups, regions, slots),
        out_shape=jax.ShapeDtypeStruct((members, levels, length), BF16),
        in_specs=[pl.BlockSpec(memory_space=pl.ANY)] + [vmem] * 7,
        out_specs=vmem,
        scratch_shapes=[
            pltpu.VMEM((rows, length), F32),
            pltpu.VMEM((STEPS, rows, length + 2 * RIM), BF16),
            pltpu.VMEM((length // RIM, 3 * RIM, RIM), BF16),
            pltpu.VMEM((groups, levels, members, PATCH_CELLS), BF16),
            pltpu.VMEM((levels, members_all, PATCH_CELLS), BF16),
            pltpu.VMEM((groups, regions, slots, 128), F32),
            pltpu.VMEM((groups, regions, slots, 128), F32),
            pltpu.VMEM((regions, 8, -(-groups * slots // 128) * 128), F32),
            pltpu.VMEM((regions, 8, -(-groups * slots // 128) * 128), F32),
            pltpu.VMEM((levels, members_all, PATCH_CELLS), BF16),
            pltpu.VMEM((groups, levels, members, PATCH_CELLS), BF16),
            pltpu.VMEM((members, levels, length), F32),
            dma((STEPS, CHUNKS, 2)), dma((STEPS, CHUNKS, 2)),
            dma((groups,)), dma((groups,)),
            dma((regions,)), dma((regions,)),
            dma((groups, CHUNKS)), dma((groups, CHUNKS)),
            dma((groups, PARTS)), dma((groups, PARTS)),
            dma((length // RIM,)),
        ],
        compiler_params=pltpu.CompilerParams(
            collective_id=0, has_side_effects=True, vmem_limit_bytes=56 * 1024 * 1024
        ),
    )(
        state, adjacent_columns, adjacent_rates, amplification_speed[None, :],
        obs_patch[None, :], obs_row[None, :], obs_value[None, :], obs_error[None, :],
    )


def solution(mesh):
    return jax.shard_map(
        on_device,
        mesh=mesh,
        in_specs=(
            P("member", None, "region"),
            P(None, "region"),
            P(None, "region"),
            P("region"),
            P(("member", "region")),
            P(("member", "region")),
            P(("member", "region")),
            P(("member", "region")),
        ),
        out_specs=P("member", None, "region"),
        check_vma=False,
    )
```
